32 devices in a mesh: groups: 2 (over y), head: 4 (over z), state: 4 (over x, core).
Axes of the slice: x: 2, y: 2, z: 4, core: 2. Of those that a mesh axis runs over, the one named last changes fastest.
Arguments:
- tokens: bfloat16 [32, 2048], P(('groups', 'head'), 'state'), parts along dimension 0, may hold values from -20 to 20
- mixer_norm: float32 [2048], P('state'), may hold values from 0.1 to 1.9
- input_proj: bfloat16 [2, 2048, 8192], P(None, 'state', 'head'), may hold values from -0.125 to 0.125
- conv_weight: float32 [4, 8192], P(None, 'head'), may hold values from -3 to 3
- conv_bias: float32 [8192], P('head'), may hold values from -3 to 3
- conv_state: float32 [3, 32, 8192], P(None, 'groups', 'head'), parts along dimension 1, may hold values from -6 to 6
- state_proj: bfloat16 [8192, 288], P('head'), may hold values from -0.125 to 0.125
- step_gain: float32 [256], replicated, may hold values from 0.1 to 1.9
- step_proj: bfloat16 [256, 8192], P(None, 'head'), may hold values from -0.375 to 0.375
- step_bias: float32 [8192], P('head'), may hold values from -6 to -1
- decay_log: float32 [16, 8192], P('state', 'head'), may hold values from 0 to 2.77
- skip_gain: float32 [8192], P('head'), may hold values from 0.5 to 1.5
- ssm_state: float32 [16, 32, 8192], P('state', 'groups', 'head'), parts along dimension 1, may hold values from -6 to 6
- output_proj: bfloat16 [8192, 2048], P('head', 'state'), may hold values from -0.0625 to 0.0625
- moe_norm: float32 [2048], replicated, may hold values from 0.1 to 1.9
- router_weight: float32 [2048, 8], replicated, may hold values from -0.125 to 0.125
- expert_ids: int32 [32, 2], P(('groups', 'head')), parts along dimension 0, may hold values from 0 to 7, as said below
- slot_ids: int32 [32, 2], P(('groups', 'head')), parts along dimension 0, may hold values from 0 to 3, as said below
- gate_proj: bfloat16 [8, 2048, 7168], P('head', None, 'state'), may hold values from -0.125 to 0.125
- up_proj: bfloat16 [8, 2048, 7168], P('head', None, 'state'), may hold values from -0.125 to 0.125
- down_proj: bfloat16 [8, 7168, 2048], P('head', 'state'), may hold values from -0.0625 to 0.0625
Outputs:
- layer_out: bfloat16 [32, 2048], P(('groups', 'head'), 'state'), parts along dimension 0
- new_conv: float32 [3, 32, 8192], P(None, 'groups', 'head'), parts along dimension 1
- new_state: float32 [16, 32, 8192], P('state', 'groups', 'head'), parts along dimension 1
- expert_load: float32 [16], P('groups'), parts along dimension 0
- aux_loss: float32 [2], P('groups'), parts along dimension 0
The draws below stay inside these ranges and needn't reach their ends.
There are 2 independent parts, one for each index of `groups`. The reference program is written for one: setup_inputs(seed, part) draws one part's arguments, and reference() takes and returns one part's arrays. A program takes and returns all parts, laid end to end along the dimension named above; an argument that names none is the same for every part. Nothing has to cross between parts.
Inputs may be any that keep to these rules, and one draw needn't show every extreme that they name: `expert_ids`: each row names 2 different experts. One expert, the same on every device, is named by every row. `slot_ids`: among the choices of one aligned block of 4 rows that name one expert, the slot positions are distinct and run from 0 to their count less one.
All inputs are finite; a program needn't handle non-finite values.
Results may differ from the reference program's by a relative error of at most 0.007.
Values may be sent and summed in bfloat16 or wider, within the bound.
No kernel may reach another device: no remote copies, remote signals or barrier semaphores. Data moves between devices by JAX's collectives and lax.ppermute only.
A program may use at most 128 MiB of HBM per device.

```python
import math
import jax
import jax.numpy as jnp
from jax import lax

D = 2048
D_INNER = 8192
D_STATE = 16
DT_RANK = 256
CONV = 4
EXPERTS = 8
TOPK = 2
FF = 7168
SEQ_DEV = 4
BATCH = 16
CAP = 2
SPLIT = 1
EXP_ROWS = 8
FF_PART = 7168


def routing_pair(key):
    base_key = jax.random.fold_in(key, 11)
    key_hot = jax.random.fold_in(base_key, 0)
    key_score = jax.random.fold_in(base_key, 2)
    key_prio = jax.random.fold_in(base_key, 3)
    blocks = BATCH // SEQ_DEV
    assigned = SEQ_DEV * TOPK
    hot_expert = jax.random.randint(key_hot, (), 0, EXPERTS)
    expert_score = jax.random.randint(key_score, (blocks, SEQ_DEV, EXPERTS), 0, 1 << 20) * EXPERTS + jnp.arange(EXPERTS, dtype=jnp.int32)
    is_hot = jnp.arange(EXPERTS, dtype=jnp.int32) == hot_expert
    expert_score = jnp.where(is_hot[None, None, :], expert_score + (1 << 30), expert_score)
    chosen_ids = lax.top_k(expert_score, TOPK)[1].astype(jnp.int32)
    flat_ids = chosen_ids.reshape(blocks, assigned)
    priority = jax.random.randint(key_prio, (blocks, assigned), 0, 1 << 20) * assigned + jnp.arange(assigned, dtype=jnp.int32)
    earlier = (flat_ids[:, :, None] == flat_ids[:, None, :]) & (priority[:, None, :] < priority[:, :, None])
    slot_pos = jnp.sum(earlier.astype(jnp.int32), axis=2)
    return (chosen_ids.reshape(BATCH, TOPK), slot_pos.reshape(BATCH, TOPK).astype(jnp.int32))


def draw_expert_ids(key, part):
    return routing_pair(key)[0]


def draw_slot_ids(key, part):
    return routing_pair(key)[1]


def draw_tokens(key, part):
    base_key = jax.random.fold_in(key, 5)
    key_scale, key_value = jax.random.split(base_key, 2)
    row_scale = jnp.exp(jax.random.uniform(key_scale, (BATCH, 1), jnp.float32, math.log(0.3), math.log(3.0)))
    values = jax.random.normal(key_value, (BATCH, D), jnp.float32)
    return jnp.clip(values * row_scale, -20.0, 20.0).astype(jnp.bfloat16)


def block_scale(rng, dims, cuts, low, top_value):
    def one(position, blocks):
        heights = jax.random.uniform(jax.random.fold_in(jax.random.fold_in(rng, 6), position), (blocks,), jnp.float32, low / len(cuts), top_value / len(cuts))
        return jnp.repeat(jnp.exp(heights), dims[position] // blocks).reshape((-1,) + (1,) * (len(dims) - position - 1))

    loudness = one(*cuts[0])
    for cut in cuts[1:]:
        loudness = loudness * one(*cut)
    return loudness


def noise(rng, shape, spread, most, cuts=(), held_as=jnp.bfloat16):
    entries = jax.random.normal(rng, shape, jnp.float32) * spread
    if len(cuts) > 0:
        entries = block_scale(rng, shape, cuts, -0.22, 0.18) * entries
    return jnp.clip(entries, min=-most, max=most).astype(held_as)


def setup_inputs(seed: int = 0, part: int = 0) -> dict:
    key_list = jax.random.split(jax.random.key(seed), 22)
    own_keys = jax.random.split(jax.random.fold_in(key_list[21], part), 22)
    return {
        "tokens": draw_tokens(jax.random.fold_in(jax.random.fold_in(key_list[21], part), 71), part),
        "mixer_norm": jnp.clip(1.0 + 0.18 * jax.random.normal(key_list[1], (D,), jnp.float32), 0.1, 1.9),
        "input_proj": noise(key_list[2], (2, D, D_INNER), D ** -0.5, 0.125, ((1, 4), (2, 4))),
        "conv_weight": noise(key_list[3], (CONV, D_INNER), CONV ** -0.5, 3.0, ((1, 4),), jnp.float32),
        "conv_bias": noise(key_list[4], (D_INNER,), 0.5, 3.0, ((0, 4),), jnp.float32),
        "conv_state": noise(own_keys[5], (CONV - 1, BATCH, D_INNER), 1.0, 6.0, ((2, 4),), jnp.float32),
        "state_proj": noise(key_list[6], (D_INNER, DT_RANK + 2 * D_STATE), (D_INNER // 4) ** -0.5, 0.125, ((0, 4),)),
        "step_gain": jnp.clip(1.0 + 0.18 * jax.random.normal(key_list[7], (DT_RANK,), jnp.float32), 0.1, 1.9),
        "step_proj": noise(key_list[8], (DT_RANK, D_INNER), DT_RANK ** -0.5, 0.375, ((1, 4),)),
        "step_bias": jnp.clip(-6.0 + 5.0 * jax.random.uniform(key_list[9], (D_INNER,), jnp.float32) ** block_scale(key_list[9], (D_INNER,), ((0, 4),), -0.2, 0.2), -6.0, -1.0),
        "decay_log": jnp.clip(2.77 * jax.random.uniform(key_list[10], (D_STATE, D_INNER), jnp.float32) ** block_scale(key_list[10], (D_STATE, D_INNER), ((0, 4), (1, 4)), -0.2, 0.2), 0.0, 2.77),
        "skip_gain": jnp.clip(0.5 + 1.0 * jax.random.uniform(key_list[11], (D_INNER,), jnp.float32) ** block_scale(key_list[11], (D_INNER,), ((0, 4),), -0.2, 0.2), 0.5, 1.5),
        "ssm_state": noise(own_keys[12], (D_STATE, BATCH, D_INNER), 1.0, 6.0, ((0, 4), (2, 4)), jnp.float32),
        "output_proj": noise(key_list[13], (D_INNER, D), D_INNER ** -0.5, 0.0625, ((0, 4), (1, 4))),
        "moe_norm": jnp.clip(1.0 + 0.18 * jax.random.normal(key_list[14], (D,), jnp.float32), 0.1, 1.9),
        "router_weight": noise(key_list[15], (D, EXPERTS), D ** -0.5, 0.125, (), jnp.float32),
        "expert_ids": draw_expert_ids(jax.random.fold_in(jax.random.fold_in(key_list[21], part), 71), part),
        "slot_ids": draw_slot_ids(jax.random.fold_in(jax.random.fold_in(key_list[21], part), 71), part),
        "gate_proj": noise(key_list[18], (EXP_ROWS, D, FF_PART), D ** -0.5, 0.125, ((0, 4), (2, 4))),
        "up_proj": noise(key_list[19], (EXP_ROWS, D, FF_PART), D ** -0.5, 0.125, ((0, 4), (2, 4))),
        "down_proj": noise(key_list[20], (EXP_ROWS, FF_PART, D), FF ** -0.5, 0.0625, ((0, 4), (1, 4))),
    }


def reference(tokens, mixer_norm, input_proj, conv_weight, conv_bias, conv_state, state_proj, step_gain, step_proj, step_bias, decay_log, skip_gain, ssm_state, output_proj, moe_norm, router_weight, expert_ids, slot_ids, gate_proj, up_proj, down_proj):
    tok_f32 = tokens.astype(jnp.float32)
    inv_first = lax.rsqrt(lax.optimization_barrier(jnp.mean(tok_f32 * tok_f32, axis=1, keepdims=True)) + 1e-05)
    normed = (tok_f32 * inv_first * mixer_norm).astype(jnp.bfloat16)
    conv_input = jnp.dot(normed, input_proj[0], preferred_element_type=jnp.float32)
    gate_branch = jnp.dot(normed, input_proj[1], preferred_element_type=jnp.float32)
    window = jnp.concatenate([conv_state, conv_input[None]], axis=0)
    conv_out = jax.nn.silu(lax.optimization_barrier(jnp.sum(conv_weight[:, None, :] * window, axis=0)) + conv_bias)
    new_conv = window[1:]
    projected = jnp.dot(conv_out.astype(jnp.bfloat16), state_proj, preferred_element_type=jnp.float32)
    step_low = projected[:, :DT_RANK]
    b_input = projected[:, DT_RANK:DT_RANK + D_STATE]
    c_output = projected[:, DT_RANK + D_STATE:]
    step_inv = lax.rsqrt(lax.optimization_barrier(jnp.mean(step_low * step_low, axis=1, keepdims=True)) + 1e-06)
    step_normed = (step_low * step_inv * step_gain).astype(jnp.bfloat16)
    step_size = jax.nn.softplus(jnp.dot(step_normed, step_proj, preferred_element_type=jnp.float32) + step_bias)
    decay_rate = jnp.exp(-step_size[None] * jnp.exp(decay_log)[:, None, :])
    new_state = decay_rate * ssm_state + step_size[None] * b_input.T[:, :, None] * conv_out[None]
    readout = lax.optimization_barrier(jnp.sum(c_output.T[:, :, None] * new_state, axis=0))
    mixer_act = ((readout + skip_gain * conv_out) * jax.nn.silu(gate_branch)).astype(jnp.bfloat16)
    residual = (tok_f32 + jnp.dot(mixer_act, output_proj, preferred_element_type=jnp.float32)).astype(jnp.bfloat16)
    resid_f32 = residual.astype(jnp.float32)
    inv_second = lax.rsqrt(lax.optimization_barrier(jnp.mean(resid_f32 * resid_f32, axis=1, keepdims=True)) + 1e-05)
    scaled = resid_f32 * moe_norm
    row_normed = (scaled * inv_second).astype(jnp.bfloat16)
    logits = inv_second * jnp.dot(scaled, router_weight, precision=lax.Precision.HIGHEST)
    expert_hit = expert_ids[:, :, None] == jnp.arange(EXPERTS, dtype=jnp.int32)[None, None, :]
    chosen = lax.optimization_barrier(jnp.sum(jnp.where(expert_hit, logits[:, None, :], 0.0), axis=2))
    gate_probs = jax.nn.sigmoid(chosen - chosen[:, ::-1])
    kept_mask = slot_ids < CAP
    mix_weight = jnp.where(kept_mask, gate_probs, 0.0)
    token_weight = lax.optimization_barrier(jnp.sum(jnp.where(expert_hit, mix_weight[:, :, None], 0.0), axis=1))
    gate_all = gate_proj.reshape(EXPERTS, SPLIT, D, FF_PART).transpose(0, 2, 1, 3).reshape(EXPERTS, D, SPLIT * FF_PART)
    up_all = up_proj.reshape(EXPERTS, SPLIT, D, FF_PART).transpose(0, 2, 1, 3).reshape(EXPERTS, D, SPLIT * FF_PART)
    down_all = down_proj.reshape(EXPERTS, SPLIT * FF_PART, D)

    def one_expert(carry, inputs):
        gate_one, up_one, down_one, weight_one = inputs
        gate_val = jnp.dot(row_normed, gate_one, preferred_element_type=jnp.float32)
        up_val = jnp.dot(row_normed, up_one, preferred_element_type=jnp.float32)
        hidden = (jax.nn.silu(gate_val) * up_val).astype(jnp.bfloat16)
        expert_value = jnp.dot(hidden, down_one, preferred_element_type=jnp.float32)
        return (carry + weight_one[:, None] * expert_value, None)
    expert_mix, _ = lax.scan(one_expert, jnp.zeros((BATCH, D), jnp.float32), (gate_all, up_all, down_all, token_weight.T))
    layer_out = (resid_f32 + expert_mix).astype(jnp.bfloat16)
    expert_load = lax.optimization_barrier(jnp.sum(jnp.where(expert_hit & kept_mask[:, :, None], 1.0, 0.0), axis=(0, 1))).astype(jnp.float32)
    mean_prob = lax.optimization_barrier(jnp.mean(jax.nn.sigmoid(logits), axis=0))
    aux_loss = (EXPERTS * jnp.sum(expert_load / (BATCH * TOPK) * mean_prob)).reshape(1)
    return (layer_out, new_conv, new_state, expert_load, aux_loss)
```

```python
import jax
import jax.numpy as jnp
from jax import lax
from jax.sharding import PartitionSpec as P

TOPK = 2
CAP = 2

NORM_EPS = 1e-05
STEP_EPS = 1e-06
LANES = 128
BF16 = jnp.bfloat16
F32 = jnp.float32


def gather_rows(block, axis):
    count = lax.axis_size(axis)
    if count > 8:
        return lax.all_gather(block, axis, axis=0, tiled=True)
    spread = jnp.broadcast_to(block[None], (count, *block.shape))
    spread = lax.all_to_all(spread, axis, split_axis=0, concat_axis=0, tiled=True)
    return spread.reshape(count * block.shape[0], *block.shape[1:])


def exchange_sum(part, axis, dtype):
    count = lax.axis_size(axis)
    if count != 4:
        return lax.psum(part, axis)
    sent = part.astype(dtype)
    others = [
        lax.ppermute(sent, axis, [(i, i ^ k) for i in range(count)]).astype(F32)
        for k in range(1, count)
    ]
    return (sent.astype(F32) + others[0]) + (others[1] + others[2])


def per_device(
    tokens,
    mixer_norm,
    input_proj,
    conv_weight,
    conv_bias,
    conv_state,
    state_proj,
    step_gain,
    step_proj,
    step_bias,
    decay_log,
    skip_gain,
    ssm_state,
    output_proj,
    moe_norm,
    router_weight,
    expert_ids,
    slot_ids,
    gate_proj,
    up_proj,
    down_proj,
):
    head_count = lax.axis_size("head")
    state_count = lax.axis_size("state")
    head_index = lax.axis_index("head")
    state_index = lax.axis_index("state")
    own_rows, own_cols = tokens.shape
    model_width = moe_norm.shape[0]
    experts = router_weight.shape[1]
    dt_rank = step_gain.shape[0]
    state_slab = decay_log.shape[0]
    d_state = state_slab * state_count
    channels = conv_bias.shape[0]

    routing = jnp.concatenate([expert_ids, jnp.minimum(slot_ids, CAP)], axis=1).astype(BF16)
    routing = jnp.pad(routing, ((0, 0), (0, LANES - 2 * TOPK)))
    packed = gather_rows(jnp.concatenate([tokens, routing], axis=1), "head")
    tok_all = packed[:, :own_cols]
    rows = tok_all.shape[0]
    expert_all = packed[:, own_cols : own_cols + TOPK].astype(jnp.int32)
    kept_all = packed[:, own_cols + TOPK : own_cols + 2 * TOPK].astype(F32) < CAP

    tok_f32 = tok_all.astype(F32)
    sq_part = jnp.sum(tok_f32 * tok_f32, axis=1, keepdims=True)
    sq_high = sq_part.astype(BF16)
    sq_low = (sq_part - sq_high.astype(F32)).astype(BF16)
    tok_gained = (tok_f32 * mixer_norm).astype(BF16)
    branch_part = jnp.einsum("td,kdc->ktc", tok_gained, input_proj, preferred_element_type=F32)
    extra = jnp.pad(jnp.concatenate([sq_high, sq_low], axis=1), ((0, 0), (0, LANES - 2)))
    extra = jnp.broadcast_to(extra[None], (2, rows, LANES))
    branch_sent = jnp.concatenate([branch_part.astype(BF16), extra], axis=2)
    branch_all = lax.all_gather(branch_sent, "state").astype(F32)
    branch_full = jnp.sum(branch_all, axis=0)
    first_sq = branch_full[0, :, channels : channels + 1] + branch_full[0, :, channels + 1 : channels + 2]
    inv_first = lax.rsqrt(first_sq / model_width + NORM_EPS)
    conv_input = branch_full[0, :, :channels] * inv_first
    gate_branch = branch_full[1, :, :channels] * inv_first
    window = jnp.concatenate([conv_state, conv_input[None]], axis=0)
    conv_out = jax.nn.silu(jnp.sum(conv_weight[:, None, :] * window, axis=0) + conv_bias)
    new_conv = window[1:]

    proj_part = jnp.dot(conv_out.astype(BF16), state_proj, preferred_element_type=F32)
    projected = exchange_sum(proj_part, "head", F32)
    step_low = projected[:, :dt_rank]
    b_input = lax.dynamic_slice_in_dim(projected, dt_rank + state_index * state_slab, state_slab, 1)
    c_output = lax.dynamic_slice_in_dim(
        projected, dt_rank + d_state + state_index * state_slab, state_slab, 1
    )
    step_inv = lax.rsqrt(jnp.mean(step_low * step_low, axis=1, keepdims=True) + STEP_EPS)
    step_normed = (step_low * step_inv * step_gain).astype(BF16)
    step_size = jax.nn.softplus(
        jnp.dot(step_normed, step_proj, preferred_element_type=F32) + step_bias
    )
    decay_rate = jnp.exp(-step_size[None] * jnp.exp(decay_log)[:, None, :])
    new_state = decay_rate * ssm_state + step_size[None] * b_input.T[:, :, None] * conv_out[None]
    read_part = jnp.sum(c_output.T[:, :, None] * new_state, axis=0)
    readout = jnp.sum(lax.all_gather(read_part.astype(BF16), "state").astype(F32), axis=0)
    mixer_act = ((readout + skip_gain * conv_out) * jax.nn.silu(gate_branch)).astype(BF16)

    mixer_sum = exchange_sum(
        jnp.dot(mixer_act, output_proj, preferred_element_type=F32), "head", BF16
    )
    resid_cols = (tok_f32 + mixer_sum).astype(BF16)
    resid_all = lax.all_gather(resid_cols, "state", axis=1, tiled=True).astype(F32)
    inv_second = lax.rsqrt(jnp.mean(resid_all * resid_all, axis=1, keepdims=True) + NORM_EPS)
    scaled = resid_all * moe_norm
    row_normed = (scaled * inv_second).astype(BF16)

    gate_val = jnp.einsum("td,ldf->ltf", row_normed, gate_proj, preferred_element_type=F32)
    up_val = jnp.einsum("td,ldf->ltf", row_normed, up_proj, preferred_element_type=F32)
    hidden = (jax.nn.silu(gate_val) * up_val).astype(BF16)
    value = jnp.einsum("ltf,lfd->ltd", hidden, down_proj, preferred_element_type=F32)

    logits = inv_second * jnp.dot(scaled, router_weight, precision=lax.Precision.HIGHEST)
    expert_hit = expert_all[:, :, None] == jnp.arange(experts, dtype=jnp.int32)[None, None, :]
    chosen = jnp.sum(jnp.where(expert_hit, logits[:, None, :], 0.0), axis=2)
    gate_probs = jax.nn.sigmoid(chosen - chosen[:, ::-1])
    mix_weight = jnp.where(kept_all, gate_probs, 0.0)
    local_experts = gate_proj.shape[0]
    split = head_count * local_experts // experts
    own_experts = (head_index * local_experts + jnp.arange(local_experts, dtype=jnp.int32)) // split
    own_hit = expert_all[None, :, :] == own_experts[:, None, None]
    own_weight = jnp.sum(jnp.where(own_hit, mix_weight[None], 0.0), axis=2)
    mix_part = jnp.sum(own_weight[:, :, None] * value, axis=0).astype(BF16)

    outgoing = mix_part.reshape(head_count, own_rows, state_count, own_cols)
    outgoing = outgoing.transpose(0, 2, 1, 3).reshape(head_count * state_count, own_rows, own_cols)
    returned = lax.all_to_all(
        outgoing, ("head", "state"), split_axis=0, concat_axis=0, tiled=True
    )
    expert_mix = jnp.sum(returned.astype(F32), axis=0)
    resid_own = lax.dynamic_slice_in_dim(resid_cols, head_index * own_rows, own_rows, 0)
    layer_out = (resid_own.astype(F32) + expert_mix).astype(BF16)

    load_sum = jnp.sum(jnp.where(expert_hit & kept_all[:, :, None], 1.0, 0.0), axis=(0, 1)).astype(
        F32
    )
    prob_sum = jnp.sum(jax.nn.sigmoid(logits), axis=0)
    aux_value = experts * jnp.sum(load_sum / (rows * TOPK) * (prob_sum / rows))
    return (layer_out, new_conv, new_state, load_sum, aux_value.reshape(1))


def solution(mesh):
    return jax.shard_map(
        per_device,
        mesh=mesh,
        in_specs=(
            P(("groups", "head"), "state"),
            P("state"),
            P(None, "state", "head"),
            P(None, "head"),
            P("head"),
            P(None, "groups", "head"),
            P("head", None),
            P(),
            P(None, "head"),
            P("head"),
            P("state", "head"),
            P("head"),
            P("state", "groups", "head"),
            P("head", "state"),
            P(),
            P(),
            P(("groups", "head"), None),
            P(("groups", "head"), None),
            P("head", None, "state"),
            P("head", None, "state"),
            P("head", "state", None),
        ),
        out_specs=(
            P(("groups", "head"), "state"),
            P(None, "groups", "head"),
            P("state", "groups", "head"),
            P("groups"),
            P("groups"),
        ),
        check_vma=False,
    )
```

```python
import functools

import jax
import jax.numpy as jnp
from jax import lax
from jax.experimental import pallas as pl
from jax.experimental.pallas import tpu as pltpu
from jax.sharding import PartitionSpec as P

TOPK = 2
CAP = 2

NORM_EPS = 1e-05
STEP_EPS = 1e-06
LANES = 128
KERNEL_VMEM = 12 * 2**20
COVER_COST = pl.CostEstimate(flops=2 * 10**10, bytes_accessed=10**8, transcendentals=0)
BF16 = jnp.bfloat16
F32 = jnp.float32


def in_vmem(array):
    return pltpu.with_memory_space_constraint(array, pltpu.VMEM)


def pack_kernel(tok_ref, ids_ref, slot_ref, out_ref):
    copies, rows, _ = out_ref.shape
    cols = tok_ref.shape[1]
    lane = lax.broadcasted_iota(jnp.int32, (rows, LANES), 1)
    routing = jnp.zeros((rows, LANES), jnp.int32)
    for k in range(TOPK):
        routing = jnp.where(lane == k, ids_ref[:, k : k + 1], routing)
        slot = jnp.minimum(slot_ref[:, k : k + 1], CAP)
        routing = jnp.where(lane == TOPK + k, slot, routing)
    routing = routing.astype(F32).astype(BF16)
    for c in range(copies):
        out_ref[c, :, :cols] = tok_ref[...]
        out_ref[c, :, cols:] = routing


def gather_tokens(tokens, expert_ids, slot_ids, axis):
    count = lax.axis_size(axis)
    rows, cols = tokens.shape
    direct = count > 8
    spread = pl.pallas_call(
        pack_kernel,
        out_shape=jax.ShapeDtypeStruct((1 if direct else count, rows, cols + LANES), BF16),
        compiler_params=pltpu.CompilerParams(vmem_limit_bytes=KERNEL_VMEM),
        cost_estimate=COVER_COST,
        name="pack",
    )(tokens, expert_ids, slot_ids)
    if direct:
        return lax.all_gather(spread[0], axis, axis=0, tiled=True)
    spread = lax.all_to_all(spread, axis, split_axis=0, concat_axis=0, tiled=True)
    return spread.reshape(count * rows, cols + LANES)


def state_kernel(
    index_ref, proj_ref, *refs, n_parts, dt_rank, d_state
):
    part_refs = refs[: n_parts - 1]
    (gain_ref, step_ref, bias_ref, decay_ref, ssm_ref, conv_ref, new_ref, read_ref) = refs[
        n_parts - 1 :
    ]
    projected = proj_ref[...]
    if n_parts == 4:
        projected = (projected + part_refs[0][...]) + (part_refs[1][...] + part_refs[2][...])
    low = projected[:, :dt_rank]
    vectors = projected[:, dt_rank:]
    inv = lax.rsqrt(jnp.mean(low * low, axis=1, keepdims=True) + STEP_EPS)
    step_normed = (low * inv * gain_ref[...]).astype(BF16)
    slab, rows, channels = ssm_ref.shape
    first = index_ref[0] * slab
    lane = lax.broadcasted_iota(jnp.int32, vectors.shape, 1)

    def column(at):
        return jnp.sum(jnp.where(lane == at, vectors, 0.0), axis=1, keepdims=True)

    b_cols = [column(first + n) for n in range(slab)]
    c_cols = [column(d_state + first + n) for n in range(slab)]
    chunk = min(channels, 256)
    for at in range(0, channels, chunk):
        span = slice(at, at + chunk)
        pre = jnp.dot(step_normed, step_ref[:, span], preferred_element_type=F32)
        pre = pre + bias_ref[:, span]
        step = jnp.maximum(pre, 0.0) + jnp.log1p(jnp.exp(-jnp.abs(pre)))
        rate = jnp.exp(decay_ref[:, span])
        step_conv = step * conv_ref[:, span]
        read = jnp.zeros((rows, chunk), F32)
        for n in range(slab):
            fresh = jnp.exp(-step * rate[n : n + 1]) * ssm_ref[n, :, span] + b_cols[n] * step_conv
            new_ref[n, :, span] = fresh
            read = read + c_cols[n] * fresh
        read_ref[:, span] = read.astype(BF16)


def experts_kernel(
    own_ref, resid_ref, route_ref, norm_ref, router_ref, gate_ref, up_ref, down_ref,
    out_ref, logit_ref, acc_ref, hidden_ref, held_ref, sems,
):
    local, _, hidden_units = gate_ref.shape
    chunk = 256 if hidden_units % 256 == 0 else hidden_units
    copies = []
    for e in range(local):
        copies.append(pltpu.make_async_copy(down_ref.at[e], held_ref.at[e], sems.at[e]))
        copies[e].start()
    blocks, own_rows, own_cols = out_ref.shape
    rows, width = resid_ref.shape
    states = width // own_cols
    resid = resid_ref[...].astype(F32)
    inv = lax.rsqrt(jnp.mean(resid * resid, axis=1, keepdims=True) + NORM_EPS)
    scaled = resid * norm_ref[...]
    logits = inv * jnp.dot(
        scaled, router_ref[...], precision=lax.Precision.HIGHEST, preferred_element_type=F32
    )
    logit_ref[...] = logits
    row_normed = (scaled * inv).astype(BF16)
    route = route_ref[...].astype(F32)
    lane = lax.broadcasted_iota(jnp.int32, logits.shape, 1)
    picks = [route[:, k : k + 1].astype(jnp.int32) for k in range(TOPK)]
    kept = [route[:, TOPK + k : TOPK + k + 1] < CAP for k in range(TOPK)]
    chosen = [jnp.sum(jnp.where(lane == p, logits, 0.0), axis=1, keepdims=True) for p in picks]
    mix = [
        jnp.where(kept[k], jax.nn.sigmoid(chosen[k] - chosen[1 - k]), 0.0) for k in range(TOPK)
    ]
    for e in range(local):
        for at in range(0, hidden_units, chunk):
            span = slice(at, at + chunk)
            gate = jnp.dot(row_normed, gate_ref[e, :, span], preferred_element_type=F32)
            up = jnp.dot(row_normed, up_ref[e, :, span], preferred_element_type=F32)
            hidden_ref[e, :, span] = (gate / (1.0 + jnp.exp(-gate)) * up).astype(BF16)
    for e in range(local):
        weight = jnp.zeros((rows, 1), F32)
        for k in range(TOPK):
            weight = weight + jnp.where(picks[k] == own_ref[e], mix[k], 0.0)
        copies[e].wait()
        for at in range(0, width, 512):
            span = slice(at, at + 512)
            value = weight * jnp.dot(
                hidden_ref[e], held_ref[e, :, span], preferred_element_type=F32
            )
            if e == 0:
                acc_ref[:, span] = value
            else:
                acc_ref[:, span] += value
    for b in range(blocks):
        at, col = (b // states) * own_rows, (b % states) * own_cols
        out_ref[b] = acc_ref[at : at + own_rows, col : col + own_cols].astype(BF16)


def exchange_sum(part, axis, dtype):
    count = lax.axis_size(axis)
    if count != 4:
        return lax.psum(part, axis)
    sent = part.astype(dtype)
    others = [
        lax.ppermute(sent, axis, [(i, i ^ k) for i in range(count)]).astype(F32)
        for k in range(1, count)
    ]
    return (sent.astype(F32) + others[0]) + (others[1] + others[2])


def exchange_parts(part, axis):
    count = lax.axis_size(axis)
    if count != 4:
        return (lax.psum(part, axis),)
    return (part,) + tuple(
        lax.ppermute(part, axis, [(i, i ^ k) for i in range(count)]) for k in range(1, count)
    )


def per_device(
    tokens,
    mixer_norm,
    input_proj,
    conv_weight,
    conv_bias,
    conv_state,
    state_proj,
    step_gain,
    step_proj,
    step_bias,
    decay_log,
    skip_gain,
    ssm_state,
    output_proj,
    moe_norm,
    router_weight,
    expert_ids,
    slot_ids,
    gate_proj,
    up_proj,
    down_proj,
):
    head_count = lax.axis_size("head")
    state_count = lax.axis_size("state")
    head_index = lax.axis_index("head")
    state_index = lax.axis_index("state")
    own_rows, own_cols = tokens.shape
    model_width = moe_norm.shape[0]
    experts = router_weight.shape[1]
    dt_rank = step_gain.shape[0]
    state_slab = decay_log.shape[0]
    d_state = state_slab * state_count
    channels = conv_bias.shape[0]

    packed = gather_tokens(tokens, expert_ids, slot_ids, "head")
    tok_all = packed[:, :own_cols]
    rows = tok_all.shape[0]
    expert_all = packed[:, own_cols : own_cols + TOPK].astype(jnp.int32)
    kept_all = packed[:, own_cols + TOPK : own_cols + 2 * TOPK].astype(F32) < CAP

    tok_f32 = tok_all.astype(F32)
    sq_part = jnp.sum(tok_f32 * tok_f32, axis=1, keepdims=True)
    sq_high = sq_part.astype(BF16)
    sq_low = (sq_part - sq_high.astype(F32)).astype(BF16)
    tok_gained = (tok_f32 * mixer_norm).astype(BF16)
    branch_part = jnp.einsum("td,kdc->ktc", tok_gained, input_proj, preferred_element_type=F32)
    extra = jnp.pad(jnp.concatenate([sq_high, sq_low], axis=1), ((0, 0), (0, LANES - 2)))
    extra = jnp.broadcast_to(extra[None], (2, rows, LANES))
    branch_sent = jnp.concatenate([branch_part.astype(BF16), extra], axis=2)
    branch_all = lax.all_gather(branch_sent, "state").astype(F32)
    branch_full = jnp.sum(branch_all, axis=0)
    first_sq = branch_full[0, :, channels : channels + 1] + branch_full[0, :, channels + 1 : channels + 2]
    inv_first = lax.rsqrt(first_sq / model_width + NORM_EPS)
    conv_input = branch_full[0, :, :channels] * inv_first
    gate_branch = branch_full[1, :, :channels] * inv_first
    window = jnp.concatenate([conv_state, conv_input[None]], axis=0)
    conv_out = jax.nn.silu(jnp.sum(conv_weight[:, None, :] * window, axis=0) + conv_bias)
    new_conv = window[1:]

    proj_part = jnp.dot(conv_out.astype(BF16), state_proj, preferred_element_type=F32)
    parts = exchange_parts(proj_part, "head")
    vmem = pl.BlockSpec(memory_space=pltpu.VMEM)
    smem = pl.BlockSpec(memory_space=pltpu.SMEM)
    new_state, read_part = pl.pallas_call(
        functools.partial(
            state_kernel, n_parts=len(parts), dt_rank=dt_rank, d_state=d_state
        ),
        in_specs=[smem] + [vmem] * (len(parts) + 6),
        out_shape=(
            jax.ShapeDtypeStruct(ssm_state.shape, F32),
            jax.ShapeDtypeStruct((rows, channels), BF16),
        ),
        compiler_params=pltpu.CompilerParams(vmem_limit_bytes=KERNEL_VMEM),
        cost_estimate=COVER_COST,
        name="state_step",
    )(
        state_index.reshape(1),
        *parts,
        step_gain[None],
        in_vmem(step_proj),
        step_bias[None],
        decay_log,
        in_vmem(ssm_state),
        conv_out,
    )
    readout = jnp.sum(lax.all_gather(read_part, "state").astype(F32), axis=0)
    mixer_act = ((readout + skip_gain * conv_out) * jax.nn.silu(gate_branch)).astype(BF16)

    mixer_sum = exchange_sum(
        jnp.dot(mixer_act, output_proj, preferred_element_type=F32), "head", BF16
    )
    resid_cols = (tok_f32 + mixer_sum).astype(BF16)
    resid_all = lax.all_gather(resid_cols, "state", axis=1, tiled=True)
    local_experts = gate_proj.shape[0]
    split = head_count * local_experts // experts
    own_experts = (head_index * local_experts + jnp.arange(local_experts, dtype=jnp.int32)) // split
    outgoing, logits = pl.pallas_call(
        experts_kernel,
        in_specs=[smem] + [vmem] * 6 + [pl.BlockSpec(memory_space=pltpu.HBM)],
        out_shape=(
            jax.ShapeDtypeStruct((head_count * state_count, own_rows, own_cols), BF16),
            jax.ShapeDtypeStruct((rows, experts), F32),
        ),
        scratch_shapes=[
            pltpu.VMEM((rows, model_width), F32),
            pltpu.VMEM((local_experts, rows, gate_proj.shape[2]), BF16),
            pltpu.VMEM(down_proj.shape, BF16),
            pltpu.SemaphoreType.DMA((local_experts,)),
        ],
        compiler_params=pltpu.CompilerParams(vmem_limit_bytes=2 * KERNEL_VMEM),
        name="experts",
    )(
        own_experts,
        resid_all,
        packed[:, own_cols:],
        moe_norm[None],
        router_weight,
        in_vmem(gate_proj),
        in_vmem(up_proj),
        down_proj,
    )
    returned = lax.all_to_all(
        outgoing, ("head", "state"), split_axis=0, concat_axis=0, tiled=True
    )
    expert_mix = jnp.sum(returned.astype(F32), axis=0)
    resid_own = lax.dynamic_slice_in_dim(resid_cols, head_index * own_rows, own_rows, 0)
    layer_out = (resid_own.astype(F32) + expert_mix).astype(BF16)

    expert_hit = expert_all[:, :, None] == jnp.arange(experts, dtype=jnp.int32)[None, None, :]
    load_sum = jnp.sum(jnp.where(expert_hit & kept_all[:, :, None], 1.0, 0.0), axis=(0, 1)).astype(
        F32
    )
    prob_sum = jnp.sum(jax.nn.sigmoid(logits), axis=0)
    aux_value = experts * jnp.sum(load_sum / (rows * TOPK) * (prob_sum / rows))
    return (layer_out, new_conv, new_state, load_sum, aux_value.reshape(1))


def solution(mesh):
    return jax.shard_map(
        per_device,
        mesh=mesh,
        in_specs=(
            P(("groups", "head"), "state"),
            P("state"),
            P(None, "state", "head"),
            P(None, "head"),
            P("head"),
            P(None, "groups", "head"),
            P("head", None),
            P(),
            P(None, "head"),
            P("head"),
            P("state", "head"),
            P("head"),
            P("state", "groups", "head"),
            P("head", "state"),
            P(),
            P(),
            P(("groups", "head"), None),
            P(("groups", "head"), None),
            P("head", None, "state"),
            P("head", None, "state"),
            P("head", "state", None),
        ),
        out_specs=(
            P(("groups", "head"), "state"),
            P(None, "groups", "head"),
            P("state", "groups", "head"),
            P("groups"),
            P("groups"),
        ),
        check_vma=False,
    )
```

```python
import functools

import jax
import jax.numpy as jnp
from jax import lax
from jax.experimental import pallas as pl
from jax.experimental.pallas import tpu as pltpu
from jax.sharding import PartitionSpec as P

TOPK = 2
CAP = 2

NORM_EPS = 1e-05
STEP_EPS = 1e-06
LANES = 128
KERNEL_VMEM = 12 * 2**20
COVER_COST = pl.CostEstimate(flops=2 * 10**10, bytes_accessed=10**8, transcendentals=0)
BF16 = jnp.bfloat16
F32 = jnp.float32


def in_vmem(array):
    return pltpu.with_memory_space_constraint(array, pltpu.VMEM)


def pack_kernel(tok_ref, ids_ref, slot_ref, out_ref):
    copies, rows, _ = out_ref.shape
    cols = tok_ref.shape[1]
    lane = lax.broadcasted_iota(jnp.int32, (rows, LANES), 1)
    routing = jnp.zeros((rows, LANES), jnp.int32)
    for k in range(TOPK):
        routing = jnp.where(lane == k, ids_ref[:, k : k + 1], routing)
        slot = jnp.minimum(slot_ref[:, k : k + 1], CAP)
        routing = jnp.where(lane == TOPK + k, slot, routing)
    routing = routing.astype(F32).astype(BF16)
    for c in range(copies):
        out_ref[c, :, :cols] = tok_ref[...]
        out_ref[c, :, cols:] = routing


def gather_tokens(tokens, expert_ids, slot_ids, axis):
    count = lax.axis_size(axis)
    rows, cols = tokens.shape
    direct = count > 8
    spread = pl.pallas_call(
        pack_kernel,
        out_shape=jax.ShapeDtypeStruct((1 if direct else count, rows, cols + LANES), BF16),
        compiler_params=pltpu.CompilerParams(vmem_limit_bytes=KERNEL_VMEM),
        cost_estimate=COVER_COST,
        name="pack",
    )(tokens, expert_ids, slot_ids)
    if direct:
        return lax.all_gather(spread[0], axis, axis=0, tiled=True)
    spread = lax.all_to_all(spread, axis, split_axis=0, concat_axis=0, tiled=True)
    return spread.reshape(count * rows, cols + LANES)


def state_kernel(
    index_ref, proj_ref, *refs, n_parts, dt_rank, d_state
):
    part_refs = refs[: n_parts - 1]
    (gain_ref, step_ref, bias_ref, decay_ref, ssm_ref, conv_ref, new_ref, read_ref) = refs[
        n_parts - 1 :
    ]
    projected = proj_ref[...]
    if n_parts == 4:
        projected = (projected + part_refs[0][...]) + (part_refs[1][...] + part_refs[2][...])
    low = projected[:, :dt_rank]
    vectors = projected[:, dt_rank:]
    inv = lax.rsqrt(jnp.mean(low * low, axis=1, keepdims=True) + STEP_EPS)
    step_normed = (low * inv * gain_ref[...]).astype(BF16)
    slab, rows, channels = ssm_ref.shape
    first = index_ref[0] * slab
    lane = lax.broadcasted_iota(jnp.int32, vectors.shape, 1)

    def column(at):
        return jnp.sum(jnp.where(lane == at, vectors, 0.0), axis=1, keepdims=True)

    b_cols = [column(first + n) for n in range(slab)]
    c_cols = [column(d_state + first + n) for n in range(slab)]
    chunk = min(channels, 256)
    for at in range(0, channels, chunk):
        span = slice(at, at + chunk)
        pre = jnp.dot(step_normed, step_ref[:, span], preferred_element_type=F32)
        pre = pre + bias_ref[:, span]
        step = jnp.maximum(pre, 0.0) + jnp.log1p(jnp.exp(-jnp.abs(pre)))
        rate = jnp.exp(decay_ref[:, span])
        step_conv = step * conv_ref[:, span]
        read = jnp.zeros((rows, chunk), F32)
        for n in range(slab):
            fresh = jnp.exp(-step * rate[n : n + 1]) * ssm_ref[n, :, span] + b_cols[n] * step_conv
            new_ref[n, :, span] = fresh
            read = read + c_cols[n] * fresh
        read_ref[:, span] = read.astype(BF16)


def experts_kernel(
    own_ref, resid_ref, route_ref, norm_ref, router_ref, gate_ref, up_ref, down_ref,
    out_ref, logit_ref, acc_ref, hidden_ref, held_ref, sems,
):
    local, _, hidden_units = gate_ref.shape
    chunk = 256 if hidden_units % 256 == 0 else hidden_units
    copies = []
    for e in range(local):
        copies.append(pltpu.make_async_copy(down_ref.at[e], held_ref.at[e], sems.at[e]))
        copies[e].start()
    blocks, own_rows, own_cols = out_ref.shape
    rows, width = resid_ref.shape
    states = width // own_cols
    resid = resid_ref[...].astype(F32)
    inv = lax.rsqrt(jnp.mean(resid * resid, axis=1, keepdims=True) + NORM_EPS)
    scaled = resid * norm_ref[...]
    logits = inv * jnp.dot(
        scaled, router_ref[...], precision=lax.Precision.HIGHEST, preferred_element_type=F32
    )
    logit_ref[...] = logits
    row_normed = (scaled * inv).astype(BF16)
    route = route_ref[...].astype(F32)
    lane = lax.broadcasted_iota(jnp.int32, logits.shape, 1)
    picks = [route[:, k : k + 1].astype(jnp.int32) for k in range(TOPK)]
    kept = [route[:, TOPK + k : TOPK + k + 1] < CAP for k in range(TOPK)]
    chosen = [jnp.sum(jnp.where(lane == p, logits, 0.0), axis=1, keepdims=True) for p in picks]
    mix = [
        jnp.where(kept[k], jax.nn.sigmoid(chosen[k] - chosen[1 - k]), 0.0) for k in range(TOPK)
    ]
    for e in range(local):
        for at in range(0, hidden_units, chunk):
            span = slice(at, at + chunk)
            gate = jnp.dot(row_normed, gate_ref[e, :, span], preferred_element_type=F32)
            up = jnp.dot(row_normed, up_ref[e, :, span], preferred_element_type=F32)
            hidden_ref[e, :, span] = (gate / (1.0 + jnp.exp(-gate)) * up).astype(BF16)
    for e in range(local):
        weight = jnp.zeros((rows, 1), F32)
        for k in range(TOPK):
            weight = weight + jnp.where(picks[k] == own_ref[e], mix[k], 0.0)
        copies[e].wait()
        for at in range(0, width, 512):
            span = slice(at, at + 512)
            value = weight * jnp.dot(
                hidden_ref[e], held_ref[e, :, span], preferred_element_type=F32
            )
            if e == 0:
                acc_ref[:, span] = value
            else:
                acc_ref[:, span] += value
    for b in range(blocks):
        at, col = (b // states) * own_rows, (b % states) * own_cols
        out_ref[b] = acc_ref[at : at + own_rows, col : col + own_cols].astype(BF16)


def exchange_sum(part, axis, dtype):
    count = lax.axis_size(axis)
    if count != 4:
        return lax.psum(part, axis)
    sent = part.astype(dtype)
    others = [
        lax.ppermute(sent, axis, [(i, i ^ k) for i in range(count)]).astype(F32)
        for k in range(1, count)
    ]
    return (sent.astype(F32) + others[0]) + (others[1] + others[2])


def exchange_parts(part, axis):
    count = lax.axis_size(axis)
    if count != 4:
        return (lax.psum(part, axis),)
    return (part,) + tuple(
        lax.ppermute(part, axis, [(i, i ^ k) for i in range(count)]) for k in range(1, count)
    )


def per_device(
    tokens,
    mixer_norm,
    input_proj,
    conv_weight,
    conv_bias,
    conv_state,
    state_proj,
    step_gain,
    step_proj,
    step_bias,
    decay_log,
    skip_gain,
    ssm_state,
    output_proj,
    moe_norm,
    router_weight,
    expert_ids,
    slot_ids,
    gate_proj,
    up_proj,
    down_proj,
):
    head_count = lax.axis_size("head")
    state_count = lax.axis_size("state")
    head_index = lax.axis_index("head")
    state_index = lax.axis_index("state")
    own_rows, own_cols = tokens.shape
    model_width = moe_norm.shape[0]
    experts = router_weight.shape[1]
    dt_rank = step_gain.shape[0]
    state_slab = decay_log.shape[0]
    d_state = state_slab * state_count
    channels = conv_bias.shape[0]

    packed = gather_tokens(tokens, expert_ids, slot_ids, "head")
    tok_all = packed[:, :own_cols]
    rows = tok_all.shape[0]
    expert_all = packed[:, own_cols : own_cols + TOPK].astype(jnp.int32)
    kept_all = packed[:, own_cols + TOPK : own_cols + 2 * TOPK].astype(F32) < CAP

    tok_f32 = tok_all.astype(F32)
    sq_part = jnp.sum(tok_f32 * tok_f32, axis=1, keepdims=True)
    sq_high = sq_part.astype(BF16)
    sq_low = (sq_part - sq_high.astype(F32)).astype(BF16)
    tok_gained = (tok_f32 * mixer_norm).astype(BF16)
    branch_part = jnp.einsum("td,kdc->ktc", tok_gained, input_proj, preferred_element_type=F32)
    extra = jnp.pad(jnp.concatenate([sq_high, sq_low], axis=1), ((0, 0), (0, LANES - 2)))
    extra = jnp.broadcast_to(extra[None], (2, rows, LANES))
    branch_sent = jnp.concatenate([branch_part.astype(BF16), extra], axis=2)
    branch_all = lax.all_gather(branch_sent, "state").astype(F32)
    branch_full = jnp.sum(branch_all, axis=0)
    first_sq = branch_full[0, :, channels : channels + 1] + branch_full[0, :, channels + 1 : channels + 2]
    inv_first = lax.rsqrt(first_sq / model_width + NORM_EPS)
    conv_input = branch_full[0, :, :channels] * inv_first
    gate_branch = branch_full[1, :, :channels] * inv_first
    window = jnp.concatenate([conv_state, conv_input[None]], axis=0)
    conv_out = jax.nn.silu(jnp.sum(conv_weight[:, None, :] * window, axis=0) + conv_bias)
    new_conv = window[1:]

    proj_part = jnp.dot(conv_out.astype(BF16), state_proj, preferred_element_type=F32)
    parts = exchange_parts(proj_part, "head")
    vmem = pl.BlockSpec(memory_space=pltpu.VMEM)
    smem = pl.BlockSpec(memory_space=pltpu.SMEM)
    new_state, read_part = pl.pallas_call(
        functools.partial(
            state_kernel, n_parts=len(parts), dt_rank=dt_rank, d_state=d_state
        ),
        in_specs=[smem] + [vmem] * (len(parts) + 6),
        out_shape=(
            jax.ShapeDtypeStruct(ssm_state.shape, F32),
            jax.ShapeDtypeStruct((rows, channels), BF16),
        ),
        compiler_params=pltpu.CompilerParams(vmem_limit_bytes=KERNEL_VMEM),
        cost_estimate=COVER_COST,
        name="state_step",
    )(
        state_index.reshape(1),
        *parts,
        step_gain[None],
        step_proj,
        step_bias[None],
        decay_log,
        ssm_state,
        conv_out,
    )
    readout = jnp.sum(lax.all_gather(read_part, "state").astype(F32), axis=0)
    mixer_act = ((readout + skip_gain * conv_out) * jax.nn.silu(gate_branch)).astype(BF16)

    mixer_sum = exchange_sum(
        jnp.dot(mixer_act, output_proj, preferred_element_type=F32), "head", F32
    )
    resid_cols = (tok_f32 + mixer_sum).astype(BF16)
    resid_all = lax.all_gather(resid_cols, "state", axis=1, tiled=True)
    local_experts = gate_proj.shape[0]
    split = head_count * local_experts // experts
    own_experts = (head_index * local_experts + jnp.arange(local_experts, dtype=jnp.int32)) // split
    outgoing, logits = pl.pallas_call(
        experts_kernel,
        in_specs=[smem] + [vmem] * 6 + [pl.BlockSpec(memory_space=pltpu.HBM)],
        out_shape=(
            jax.ShapeDtypeStruct((head_count * state_count, own_rows, own_cols), BF16),
            jax.ShapeDtypeStruct((rows, experts), F32),
        ),
        scratch_shapes=[
            pltpu.VMEM((rows, model_width), F32),
            pltpu.VMEM((local_experts, rows, gate_proj.shape[2]), BF16),
            pltpu.VMEM(down_proj.shape, BF16),
            pltpu.SemaphoreType.DMA((local_experts,)),
        ],
        compiler_params=pltpu.CompilerParams(vmem_limit_bytes=2 * KERNEL_VMEM),
        name="experts",
    )(
        own_experts,
        resid_all,
        packed[:, own_cols:],
        moe_norm[None],
        router_weight,
        in_vmem(gate_proj),
        in_vmem(up_proj),
        down_proj,
    )
    returned = lax.all_to_all(
        outgoing, ("head", "state"), split_axis=0, concat_axis=0, tiled=True
    )
    expert_mix = jnp.sum(returned.astype(F32), axis=0)
    resid_own = lax.dynamic_slice_in_dim(resid_cols, head_index * own_rows, own_rows, 0)
    layer_out = (resid_own.astype(F32) + expert_mix).astype(BF16)

    expert_hit = expert_all[:, :, None] == jnp.arange(experts, dtype=jnp.int32)[None, None, :]
    load_sum = jnp.sum(jnp.where(expert_hit & kept_all[:, :, None], 1.0, 0.0), axis=(0, 1)).astype(
        F32
    )
    prob_sum = jnp.sum(jax.nn.sigmoid(logits), axis=0)
    aux_value = experts * jnp.sum(load_sum / (rows * TOPK) * (prob_sum / rows))
    return (layer_out, new_conv, new_state, load_sum, aux_value.reshape(1))


def solution(mesh):
    return jax.shard_map(
        per_device,
        mesh=mesh,
        in_specs=(
            P(("groups", "head"), "state"),
            P("state"),
            P(None, "state", "head"),
            P(None, "head"),
            P("head"),
            P(None, "groups", "head"),
            P("head", None),
            P(),
            P(None, "head"),
            P("head"),
            P("state", "head"),
            P("head"),
            P("state", "groups", "head"),
            P("head", "state"),
            P(),
            P(),
            P(("groups", "head"), None),
            P(("groups", "head"), None),
            P("head", None, "state"),
            P("head", None, "state"),
            P("head", "state", None),
        ),
        out_specs=(
            P(("groups", "head"), "state"),
            P(None, "groups", "head"),
            P("state", "groups", "head"),
            P("groups"),
            P("groups"),
        ),
        check_vma=False,
    )
```
